32 devices in a mesh: gx: 2 (over core), gy: 4 (over z), gz: 4 (over y, x).
Axes of the slice: x: 2, y: 2, z: 4, core: 2. Of those that a mesh axis runs over, the one named last changes fastest.
Arguments:
- particles: float32 [28, 65536], P(None, ('gx', 'gy', 'gz')), may hold values from -3 to 3, as said below
- stencil_base: int32 [3, 65536], P(None, ('gx', 'gy', 'gz')), may hold values from 0 to 32, as said below
- weights: float32 [8, 65536], P(None, ('gx', 'gy', 'gz')), may hold values from 0.02 to 0.25
- gradients: float32 [3, 8, 65536], P(None, None, ('gx', 'gy', 'gz')), may hold values from -4 to 4
- counts: int32 [32], P(('gx', 'gy', 'gz')), may hold values from 0 to 8, as said below
Outputs:
- migrated: float32 [28, 98304], P(None, ('gx', 'gy', 'gz'))
- damage: float32 [16, 64, 128], P('gx', 'gy', 'gz')
The draws below stay inside these ranges and needn't reach their ends.
Inputs may be any that keep to these rules, and one draw needn't show every extreme that they name: `particles`: mass and volume in 0.5 to 2, deformation gradient entries within 0.1 of the identity's, damage in 0 to 0.5, history in 0.05 to 1. `stencil_base`: row 0 lies in 0 to 8, row 1 in 0 to 16, row 2 in 0 to 32. `counts`: some device hands exactly 8 bins.
All inputs are finite; a program needn't handle non-finite values.
Results may differ from the reference program's by a relative error of at most 0.0003.
Values sent between devices are 32-bit elements; how exact they have to be, the bound alone decides.
A program may use at most 64 MiB of HBM per device.

```python
import math
import jax
import jax.numpy as jnp
from jax import lax

CX = 8
CY = 16
CZ = 32
NBIN = 16
BIN = 128
SUBSTEPS = 4
FIELDS = 28
MOST = 8
RANKS = 32
PARTICLES = 65536
NX = 16
NY = 64
NZ = 128
N_GX = 2
N_GY = 4
N_GZ = 4


def draw_particles(key, part):
    keys = jax.random.split(key, 7)
    count = PARTICLES
    scales = jnp.exp(jax.random.uniform(keys[0], (2, count), jnp.float32, math.log(0.5), math.log(2.0)))
    velocity = jnp.clip(0.5 * jax.random.normal(keys[1], (3, count), jnp.float32), -2.0, 2.0)
    stress = jnp.clip(0.5 * jax.random.normal(keys[3], (9, count), jnp.float32), -3.0, 3.0)
    deform = jnp.eye(3, dtype=jnp.float32).reshape(9, 1) + jax.random.uniform(keys[2], (9, count), jnp.float32, -0.1, 0.1)
    damage = jax.random.uniform(keys[4], (1, count), jnp.float32, 0.0, 0.5)
    history = jnp.exp(jax.random.uniform(keys[5], (1, count), jnp.float32, math.log(0.05), 0.0))
    position = jax.random.uniform(keys[6], (3, count), jnp.float32, 0.0, 1.0)
    return jnp.concatenate([scales, velocity, deform, stress, damage, history, position], axis=0)


def draw_stencil_base(key, part):
    keys = jax.random.split(key, 3)
    row_x = jax.random.randint(keys[0], (PARTICLES,), 0, CX + 1)
    row_y = jax.random.randint(keys[1], (PARTICLES,), 0, CY + 1)
    row_z = jax.random.randint(keys[2], (PARTICLES,), 0, CZ + 1)
    return jnp.stack([row_x, row_y, row_z]).astype(jnp.int32)


def draw_counts(key, part):
    values = jax.random.randint(key, (RANKS,), 0, MOST + 1)
    chosen = jax.random.randint(jax.random.fold_in(key, 7), (), 0, RANKS)
    return values.at[chosen].set(MOST).astype(jnp.int32)


def level_of(key, shape, cuts, low, top_value):
    def one(axis_at, shards_of):
        draws = jax.random.uniform(jax.random.fold_in(jax.random.fold_in(key, 6), axis_at), (shards_of,), jnp.float32, low / len(cuts), top_value / len(cuts))
        return jnp.repeat(jnp.exp(draws), shape[axis_at] // shards_of).reshape((-1,) + (1,) * (len(shape) - axis_at - 1))

    level = one(*cuts[0])
    for cut in cuts[1:]:
        level = level * one(*cut)
    return level


def noise(key, dims, scale, most, shards=(), kind=jnp.bfloat16):
    result = scale * jax.random.normal(key, dims, jnp.float32)
    if shards:
        result = result * level_of(key, dims, shards, -0.22, 0.18)
    return jnp.clip(result, -most, most).astype(kind)


def setup_inputs(seed: int = 0) -> dict:
    splits = jax.random.split(jax.random.key(seed), 6)
    particles = draw_particles(jax.random.fold_in(splits[5], 71), 0)
    stencil_base = draw_stencil_base(jax.random.fold_in(splits[5], 71), 0)
    weights = jnp.clip(0.02 + 0.23 * jax.random.uniform(splits[2], (8, PARTICLES), jnp.float32) ** level_of(splits[2], (8, PARTICLES), ((1, 32),), -0.2, 0.2), 0.02, 0.25)
    gradients = noise(splits[3], (3, 8, PARTICLES), 1.0, 4.0, ((2, 32),), jnp.float32)
    counts = draw_counts(jax.random.fold_in(splits[5], 71), 0)
    return {"particles": particles, "stencil_base": stencil_base, "weights": weights, "gradients": gradients, "counts": counts}


time_step = 0.1
relax_rate = 0.2
length_sq = 0.6
shear_mod = 1.0
bulk_coef = 1.5
mass_floor = 0.5


def corner_offsets(corner):
    return (corner >> 2) & 1, (corner >> 1) & 1, corner & 1


def node_terms(particles, weights, gradients, corner):
    volume = particles[1]
    velocity = particles[2:5]
    stress = particles[14:23].reshape(3, 3, -1)
    share = particles[0] * weights[corner]
    slope = gradients[:, corner]
    force = -volume[None] * jnp.sum(stress * slope[None], axis=1)
    return jnp.concatenate([share[None], share[None] * velocity, force, (share * particles[23])[None], (share * particles[24])[None]], axis=0)


def relax(padded, drive):
    centre = padded[1:-1, 1:-1, 1:-1]
    laplace = (padded[2:, 1:-1, 1:-1] + padded[:-2, 1:-1, 1:-1] + padded[1:-1, 2:, 1:-1] + padded[1:-1, :-2, 1:-1] + padded[1:-1, 1:-1, 2:] + padded[1:-1, 1:-1, :-2]) - 6.0 * centre
    return centre + relax_rate * (length_sq * laplace - centre + 2.0 * (1.0 - centre) * drive)


def advance(particles, near_velocity, near_damage, weights, gradients):
    moved = [jnp.sum(weights * near_velocity[i], axis=0) for i in range(3)]
    velgrad = [[jnp.sum(near_velocity[i] * gradients[j], axis=0) for j in range(3)] for i in range(3)]
    damage_node = jnp.sum(weights * near_damage, axis=0)
    deform = [[particles[5 + 3 * i + j] for j in range(3)] for i in range(3)]
    stretch = [[(1.0 if i == j else 0.0) + time_step * velgrad[i][j] for j in range(3)] for i in range(3)]
    mapped = [[stretch[i][0] * deform[0][j] + stretch[i][1] * deform[1][j] + stretch[i][2] * deform[2][j] for j in range(3)] for i in range(3)]
    jacobian = (mapped[0][0] * (mapped[1][1] * mapped[2][2] - mapped[1][2] * mapped[2][1])
                - mapped[0][1] * (mapped[1][0] * mapped[2][2] - mapped[1][2] * mapped[2][0])
                + mapped[0][2] * (mapped[1][0] * mapped[2][1] - mapped[1][1] * mapped[2][0]))
    left = [[mapped[i][0] * mapped[j][0] + mapped[i][1] * mapped[j][1] + mapped[i][2] * mapped[j][2] for j in range(3)] for i in range(3)]
    damaged = jnp.maximum(particles[23], damage_node)
    degrade = (1.0 - damaged) ** 2
    rows_out = []
    for i in range(3):
        for j in range(3):
            term = shear_mod * (left[i][j] - (1.0 if i == j else 0.0))
            if i == j:
                term = term + bulk_coef * (jacobian - 1.0)
            rows_out.append(degrade * term)
    energy = 0.5 * shear_mod * (left[0][0] + left[1][1] + left[2][2] - 3.0) + 0.5 * bulk_coef * (jacobian - 1.0) ** 2
    history = jnp.maximum(particles[24], energy)
    position = particles[25:28] + time_step * jnp.stack(moved)
    flat_mapped = jnp.stack([mapped[i][j] for i in range(3) for j in range(3)])
    return jnp.concatenate([particles[0:2], jnp.stack(moved), flat_mapped, jnp.stack(rows_out), damaged[None], history[None], position], axis=0)


def assemble(own, tail, own_count, prior):
    buffer_all = jnp.concatenate([tail, own, jnp.zeros((own.shape[0], MOST * BIN), own.dtype)], axis=1)
    start = ((MOST - prior) * BIN).astype(jnp.int32)
    window = lax.dynamic_slice_in_dim(buffer_all, start, (NBIN + MOST) * BIN, 1)
    live = (NBIN - own_count + prior) * BIN
    slot = jnp.arange((NBIN + MOST) * BIN, dtype=jnp.int32)
    return jnp.where(slot[None, :] < live, window, jnp.zeros_like(window))


def reference(particles, stencil_base, weights, gradients, counts):
    per_device = NBIN * BIN
    span_y = NY + 2
    span_z = NZ + 2
    base = stencil_base.reshape(3, N_GX, N_GY, N_GZ, per_device)
    row_x = base[0] + (jnp.arange(N_GX, dtype=jnp.int32) * CX)[:, None, None, None]
    row_y = base[1] + (jnp.arange(N_GY, dtype=jnp.int32) * CY)[None, :, None, None]
    row_z = base[2] + (jnp.arange(N_GZ, dtype=jnp.int32) * CZ)[None, None, :, None]
    flats = []
    terms = []
    for corner in range(8):
        offset_x, offset_y, offset_z = corner_offsets(corner)
        flat_index = (((row_x + offset_x) * span_y + row_y + offset_y) * span_z + row_z + offset_z).reshape(-1).astype(jnp.int32)
        flats.append(flat_index)
        terms.append(node_terms(particles, weights, gradients, corner))
    all_index = jnp.concatenate(flats)
    grid_sum = jnp.zeros((9, (NX + 2) * span_y * span_z), jnp.float32).at[:, all_index].add(jnp.concatenate(terms, axis=1))
    owned = grid_sum.reshape(9, NX + 2, span_y, span_z)[:, 1:-1, 1:-1, 1:-1]
    masses = jnp.maximum(owned[0], mass_floor)
    velocity = (owned[1:4] + time_step * owned[4:7]) / masses[None]
    damage = owned[7] / masses
    drive = owned[8] / masses
    for step in range(SUBSTEPS):
        damage = relax(jnp.pad(damage, 1), drive)
    fields = jnp.pad(jnp.concatenate([velocity, damage[None]], axis=0), ((0, 0), (1, 1), (1, 1), (1, 1))).reshape(4, -1)
    near = fields[:, all_index].reshape(4, 8, PARTICLES)
    updated = advance(particles, near[0:3], near[3], weights, gradients)
    lines = N_GX * N_GY
    grouped = updated.reshape(FIELDS, lines, N_GZ, per_device)
    earlier = jnp.roll(grouped, 1, axis=2)
    tails = earlier[..., (NBIN - MOST) * BIN:]
    count_grid = counts.reshape(lines, N_GZ)
    prior = jnp.roll(count_grid, 1, axis=1)
    owns = jnp.transpose(grouped, (1, 2, 0, 3)).reshape(lines * N_GZ, FIELDS, per_device)
    tail_rows = jnp.transpose(tails, (1, 2, 0, 3)).reshape(lines * N_GZ, FIELDS, MOST * BIN)
    placed = jax.vmap(assemble)(owns, tail_rows, count_grid.reshape(-1), prior.reshape(-1))
    migrated = jnp.transpose(placed, (1, 0, 2)).reshape(FIELDS, -1)
    return migrated, damage
```

```python
import functools
import jax
import jax.numpy as jnp
from jax import lax
from jax.experimental import pallas as pl
from jax.experimental.pallas import tpu as pltpu
from jax.sharding import PartitionSpec as P

CX = 8
CY = 16
CZ = 32
NBIN = 16
BIN = 128
SUBSTEPS = 4
MOST = 8

time_step = 0.1
relax_rate = 0.2
length_sq = 0.6
shear_mod = 1.0
bulk_coef = 1.5
mass_floor = 0.5

MESH = pl.DeviceIdType.MESH


def up_to(value, unit):
    return (value + unit - 1) // unit * unit


H = SUBSTEPS + 1
SX, SY, SZ = CX + 2 * H, CY + 2 * H, CZ + 2 * H
LW = up_to(SY * SZ, 128)
NB = up_to(CY * SZ + CZ + 1, 128)
OFF = (H - 1) * SZ + H - 1
RD = up_to(SX, 8)
RV = up_to(CX + 2, 8)
XA, XB = (H - 1) * SZ // 128 * 128, up_to((H + 1 + CY) * SZ, 128)
KEEP = H + 1
XROWS = 3 * KEEP + 6
YW = up_to(KEEP * SZ, 128)
YROWS = 3 * RD + 3 * RV // 2
DT, VT = 3 * RD // 8, 3 * RV // 8
SLOTS = SZ // KEEP
PER = KEEP // 2
ZSLOTS = DT + (VT + PER - 1) // PER
ZT = (ZSLOTS + SLOTS - 1) // SLOTS
TAIL = MOST * BIN


def split(value):
    high = value.astype(jnp.bfloat16)
    low = (value - high.astype(jnp.float32)).astype(jnp.bfloat16)
    return high, low


def take(ref, lane0, width):
    a = lane0 // 128 * 128
    span = up_to(lane0 - a + width, 128)
    value = ref[:, a : a + span]
    shift = (span - (lane0 - a)) % span
    if shift:
        value = pltpu.roll(value, shift, 1)
    value = value[:, : up_to(width, 128)]
    lane = lax.broadcasted_iota(jnp.int32, value.shape, 1)
    return jnp.where(lane < width, value, 0.0)


def put_add(ref, lane0, width, value):
    a = lane0 // 128 * 128
    span = max(up_to(lane0 - a + width, 128), value.shape[1])
    extra = span - value.shape[1]
    if extra:
        value = jnp.concatenate([value, jnp.zeros((value.shape[0], extra), jnp.float32)], axis=1)
    if lane0 - a:
        value = pltpu.roll(value, lane0 - a, 1)
    ref[:, a : a + span] += value


def make_onehot(base_ref, hot):
    flat = base_ref[1:2, :] * SZ + base_ref[2:3, :]
    for r in range(0, NB, 128):
        row = lax.broadcasted_iota(jnp.int32, (128, flat.shape[1]), 0) + r
        hot[r : r + 128, :] = (row == flat).astype(jnp.float32).astype(jnp.bfloat16)


def scatter(part, base_ref, weight, slope, hot, coef, left, nodes, dref, vref, xs_low, xs_high):
    count = part.shape[1]
    mass = part[0:1, :]
    scale = -time_step * part[1:2, :]
    coef[...] = jnp.zeros_like(coef)
    coef[0:1, :] = mass
    coef[1:2, :] = mass * part[23:24, :]
    coef[2:3, :] = mass * part[24:25, :]
    coef[3:6, :] = mass * part[2:5, :]
    for j in range(3):
        for i in range(3):
            coef[8 + 8 * j + 3 + i : 8 + 8 * j + 4 + i, :] = scale * part[14 + 3 * i + j : 15 + 3 * i + j, :]
    bx = jnp.broadcast_to(base_ref[0:1, :], (8, count))
    for bc in range(4):
        pair = []
        for a in range(2):
            k = 4 * a + bc
            term = weight[k : k + 1, :] * coef[0:8, :]
            for j in range(3):
                term = term + slope[8 * j + k : 8 * j + k + 1, :] * coef[8 + 8 * j : 16 + 8 * j, :]
            high = term.astype(jnp.bfloat16).astype(jnp.float32)
            pair.append((high, term - high))
        for x in range(CX + 2):
            for s in range(2):
                row = x * 64 + s * 32 + bc * 8
                value = jnp.where(bx == x, pair[0][s], jnp.where(bx == x - 1, pair[1][s], 0.0))
                left[row : row + 8, :] = value.astype(jnp.bfloat16)
    sums = lax.dot_general(left[...], hot[...], (((1,), (1,)), ((), ())), preferred_element_type=jnp.float32)
    sums = sums.reshape(CX + 2, 2, 4, 8, NB)
    sums = sums[:, 0] + sums[:, 1]
    total = None
    for bc in range(4):
        piece = sums[:, bc].reshape((CX + 2) * 8, NB)
        piece = jnp.concatenate([piece, jnp.zeros((piece.shape[0], LW - NB), jnp.float32)], axis=1)
        piece = pltpu.roll(piece, OFF + (bc >> 1) * SZ + (bc & 1), 1)
        total = piece if total is None else total + piece
    for x in range(CX + 2):
        nodes[x] = total[8 * x : 8 * x + 8, :]
    dref[...] = jnp.zeros_like(dref)
    vref[...] = jnp.zeros_like(vref)
    for x in range(CX + 2):
        for c in range(3):
            dref[c * RD + H - 1 + x : c * RD + H + x, :] = nodes[x, c : c + 1, :]
            vref[c * RV + x : c * RV + x + 1, :] = nodes[x, 3 + c : 4 + c, :]
    for c in range(3):
        at = c * RD + H - 1
        xs_high[c * KEEP : (c + 1) * KEEP, :] = dref[at + CX + 2 - KEEP : at + CX + 2, XA:XB]
        xs_low[c * KEEP : (c + 1) * KEEP, :] = dref[at : at + KEEP, XA:XB]
        at = 3 * KEEP + 2 * c
        xs_high[at : at + 2, :] = vref[c * RV + CX : c * RV + CX + 2, XA:XB]
        xs_low[at : at + 2, :] = vref[c * RV : c * RV + 2, XA:XB]


def only(has, value):
    return jnp.where(has, value, jnp.zeros_like(value))


def add_x(dref, vref, from_low, from_high, has_low, has_high, ys_low, ys_high):
    low = only(has_low, from_low[...])
    high = only(has_high, from_high[...])
    for c in range(3):
        dref[c * RD : c * RD + KEEP, XA:XB] += low[c * KEEP : (c + 1) * KEEP]
        dref[c * RD + SX - KEEP : c * RD + SX, XA:XB] += high[c * KEEP : (c + 1) * KEEP]
        at = 3 * KEEP + 2 * c
        vref[c * RV : c * RV + 2, XA:XB] += low[at : at + 2]
        vref[c * RV + CX : c * RV + CX + 2, XA:XB] += high[at : at + 2]
    half = 3 * RV // 2
    for ys, d0, v0 in ((ys_high, CY * SZ, (H - 1 + CY) * SZ), (ys_low, (H - 1) * SZ, (H - 1) * SZ)):
        ys[: 3 * RD, :] = take(dref, d0, KEEP * SZ)
        near = take(vref, v0, 2 * SZ)
        ys[3 * RD :, 0:128] = near[:half]
        ys[3 * RD :, 128:256] = near[half:]


def lane_z():
    lane = lax.broadcasted_iota(jnp.int32, (8, LW), 1).astype(jnp.float32)
    y = jnp.floor((lane + 0.5) * (1.0 / SZ))
    return lane - SZ * y, y


def slot_of(t):
    if t < DT:
        s, sub, width = t, 0, KEEP
    else:
        s, sub, width = DT + (t - DT) // PER, 2 * ((t - DT) % PER), 2
    return s // SLOTS, (s % SLOTS) * KEEP + sub, width


def tile_of(t, dref, vref):
    return dref.at[8 * t : 8 * t + 8] if t < DT else vref.at[8 * (t - DT) : 8 * (t - DT) + 8]


def add_y(dref, vref, from_low, from_high, has_low, has_high, zs_low, zs_high):
    for got, has, d0, v0 in (
        (from_low, has_low, 0, (H - 1) * SZ),
        (from_high, has_high, (SY - KEEP) * SZ, (H - 1 + CY) * SZ),
    ):
        put_add(dref, d0, KEEP * SZ, only(has, got[: 3 * RD, :]))
        near = jnp.concatenate([got[3 * RD :, 0:128], got[3 * RD :, 128:256]], axis=0)
        put_add(vref, v0, 2 * SZ, only(has, near))
    z, _ = lane_z()
    for zs, d0, v0 in ((zs_high, CZ, H - 1 + CZ), (zs_low, H - 1, H - 1)):
        out = [None] * ZT
        for t in range(DT + VT):
            block, at, width = slot_of(t)
            shift = (at - (d0 if t < DT else v0)) % LW
            value = tile_of(t, dref, vref)[...]
            if shift:
                value = pltpu.roll(value, shift, 1)
            value = jnp.where((z >= at) & (z < at + width), value, 0.0)
            out[block] = value if out[block] is None else out[block] + value
        for block in range(ZT):
            zs[8 * block : 8 * block + 8, :] = out[block]


def add_z(dref, vref, from_low, from_high, has_low, has_high):
    z, _ = lane_z()
    for got, has, d0, v0 in (
        (from_low, has_low, 0, H - 1),
        (from_high, has_high, SZ - KEEP, H - 1 + CZ),
    ):
        for t in range(DT + VT):
            block, at, width = slot_of(t)
            value = only(has, got[8 * block : 8 * block + 8, :])
            value = jnp.where((z >= at) & (z < at + width), value, 0.0)
            shift = ((d0 if t < DT else v0) - at) % LW
            if shift:
                value = pltpu.roll(value, shift, 1)
            tile = tile_of(t, dref, vref)
            tile[...] += value


def relax_all(dref, vref, place, nodes_x, nodes_y, nodes_z, wet, fields, field_left, damage_out):
    ix, iy, iz = place
    z, y = lane_z()
    z, y = z[0:1], y[0:1]
    gz = z - H + (iz * CZ).astype(jnp.float32)
    gy = y - H + (iy * CY).astype(jnp.float32)
    flat_in = (gz >= 0) & (gz < nodes_z) & (gy >= 0) & (gy < nodes_y) & (y < SY)
    row = lax.broadcasted_iota(jnp.int32, (RD, 1), 0)
    gx = row - H + ix * CX
    row_in = (gx >= 0) & (gx < nodes_x) & (row < SX)
    inside = row_in.astype(jnp.float32) * flat_in.astype(jnp.float32)
    mass = jnp.maximum(dref[0:RD, :], mass_floor)
    damage = dref[RD : 2 * RD, :] / mass * inside
    drive = dref[2 * RD : 3 * RD, :] / mass
    wet[0:RD, :] = mass
    wet[RD : 2 * RD, :] = inside
    for _ in range(SUBSTEPS):
        ring = (
            pltpu.roll(damage, 1, 0)
            + pltpu.roll(damage, RD - 1, 0)
            + pltpu.roll(damage, SZ, 1)
            + pltpu.roll(damage, LW - SZ, 1)
            + pltpu.roll(damage, 1, 1)
            + pltpu.roll(damage, LW - 1, 1)
        )
        laplace = ring - 6.0 * damage
        damage = (damage + relax_rate * (length_sq * laplace - damage + 2.0 * (1.0 - damage) * drive)) * inside
    wet[2 * RD : 3 * RD, :] = damage
    damage_out[...] = wet[2 * RD + H : 2 * RD + H + CX, :]
    n = CX + 2
    factor = wet[RD + H - 1 : RD + H - 1 + n, :] / wet[H - 1 : H - 1 + n, :]
    fields[...] = jnp.zeros_like(fields)
    for c in range(3):
        fields[c * 16 : c * 16 + n, :] = vref[c * RV : c * RV + n, :] * factor
    fields[48 : 48 + n, :] = wet[2 * RD + H - 1 : 2 * RD + H - 1 + n, :]
    whole = fields[...]
    for bc in range(4):
        moved = pltpu.roll(whole, LW - OFF - (bc >> 1) * SZ - (bc & 1), 1)[:, :NB]
        for f in range(4):
            for x in range(n):
                r = x * 16 + f * 4 + bc
                field_left[r : r + 1, :] = moved[f * 16 + x : f * 16 + x + 1, :]


def advance(part, base_ref, weight, slope, hot, field_left, out, at, count):
    lanes = slice(at, at + count)
    n = CX + 2
    high, low = split(field_left[...])
    got = jnp.dot(high, hot[:, lanes], preferred_element_type=jnp.float32)
    got = got + jnp.dot(low, hot[:, lanes], preferred_element_type=jnp.float32)
    bx = jnp.broadcast_to(base_ref[0:1, lanes], (16, count))
    near = [jnp.zeros((16, count), jnp.float32), jnp.zeros((16, count), jnp.float32)]
    for x in range(n):
        rows = got[16 * x : 16 * x + 16]
        near[0] = jnp.where(bx == x, rows, near[0])
        near[1] = jnp.where(bx == x - 1, rows, near[1])
    w = weight[:, lanes]
    g = [slope[8 * j : 8 * j + 8, lanes] for j in range(3)]
    corner = [jnp.concatenate([near[0][4 * f : 4 * f + 4], near[1][4 * f : 4 * f + 4]], axis=0) for f in range(4)]
    total = lambda v: jnp.sum(v, axis=0, keepdims=True)
    moved = [total(w * corner[i]) for i in range(3)]
    velgrad = [[total(corner[i] * g[j]) for j in range(3)] for i in range(3)]
    damage_node = total(w * corner[3])
    p = lambda r: part[r : r + 1, lanes]
    deform = [[p(5 + 3 * i + j) for j in range(3)] for i in range(3)]
    stretch = [[(1.0 if i == j else 0.0) + time_step * velgrad[i][j] for j in range(3)] for i in range(3)]
    mapped = [
        [stretch[i][0] * deform[0][j] + stretch[i][1] * deform[1][j] + stretch[i][2] * deform[2][j] for j in range(3)]
        for i in range(3)
    ]
    jacobian = (
        mapped[0][0] * (mapped[1][1] * mapped[2][2] - mapped[1][2] * mapped[2][1])
        - mapped[0][1] * (mapped[1][0] * mapped[2][2] - mapped[1][2] * mapped[2][0])
        + mapped[0][2] * (mapped[1][0] * mapped[2][1] - mapped[1][1] * mapped[2][0])
    )
    left = {}
    for i in range(3):
        for j in range(i, 3):
            left[i, j] = mapped[i][0] * mapped[j][0] + mapped[i][1] * mapped[j][1] + mapped[i][2] * mapped[j][2]
            left[j, i] = left[i, j]
    damaged = jnp.maximum(p(23), damage_node)
    degrade = (1.0 - damaged) ** 2
    swell = bulk_coef * (jacobian - 1.0)

    def put(r, value):
        out[r : r + 1, lanes] = value

    out[0:2, lanes] = part[0:2, lanes]
    for i in range(3):
        put(2 + i, moved[i])
        put(25 + i, p(25 + i) + time_step * moved[i])
        for j in range(3):
            put(5 + 3 * i + j, mapped[i][j])
            term = shear_mod * (left[i, j] - (1.0 if i == j else 0.0))
            if i == j:
                term = term + swell
            put(14 + 3 * i + j, degrade * term)
    put(23, damaged)
    energy = 0.5 * shear_mod * (left[0, 0] + left[1, 1] + left[2, 2] - 3.0) + 0.5 * bulk_coef * (jacobian - 1.0) ** 2
    put(24, jnp.maximum(p(24), energy))


def step_kernel(
    sizes, part, base_ref, weight, slope, counts, updated, tail, damage_out,
    hot, coef, left, nodes, dref, vref, wet, fields, field_left,
    sx, rx, sy, ry, sz, rz, give, take_in, send_sem, recv_sem,
):
    names = ("gx", "gy", "gz")
    place = [lax.axis_index(a) for a in names]
    has_low = [i > 0 for i in place]
    has_high = [i < n - 1 for i, n in zip(place, sizes)]
    last = sizes[2]
    following, previous = lax.rem(place[2] + 1, last), lax.rem(place[2] + last - 1, last)
    barrier = pltpu.get_barrier_semaphore()
    waits = 2
    for k in range(2):
        for has, other in ((has_low[k], place[k] - 1), (has_high[k], place[k] + 1)):
            @pl.when(has)
            def _(k=k, other=other):
                pl.semaphore_signal(barrier, inc=1, device_id={names[k]: other}, device_id_type=MESH)
            waits = waits + has.astype(jnp.int32)
    for other in (following, previous):
        pl.semaphore_signal(barrier, inc=1, device_id={"gz": other}, device_id_type=MESH)

    make_onehot(base_ref, hot)
    scatter(part, base_ref, weight, slope, hot, coef, left, nodes, dref, vref, sx.at[0], sx.at[1])
    pl.semaphore_wait(barrier, waits)

    def copies(k, src, dst):
        made = []
        for d, other in ((0, place[k] - 1), (1, place[k] + 1)):
            made.append(pltpu.make_async_remote_copy(
                src_ref=src.at[d], dst_ref=dst.at[1 - d], send_sem=send_sem.at[k, d],
                recv_sem=recv_sem.at[k, 1 - d], device_id={names[k]: other}, device_id_type=MESH))
        return made

    def exchange(k, src, dst):
        made = copies(k, src, dst)
        ahead = ((has_low[k], made[0]), (has_high[k], made[1]))
        for has, copy in ahead:
            @pl.when(has)
            def _(copy=copy):
                copy.start()
        for has, copy in ((has_low[k], made[1]), (has_high[k], made[0])):
            @pl.when(has)
            def _(copy=copy):
                copy.wait_recv()
        for has, copy in ahead:
            @pl.when(has)
            def _(copy=copy):
                copy.wait_send()

    exchange(0, sx, rx)
    add_x(dref, vref, rx.at[0], rx.at[1], has_low[0], has_high[0], sy.at[0], sy.at[1])
    exchange(1, sy, ry)
    add_y(dref, vref, ry.at[0], ry.at[1], has_low[1], has_high[1], sz.at[0], sz.at[1])
    exchange(2, sz, rz)
    add_z(dref, vref, rz.at[0], rz.at[1], has_low[2], has_high[2])
    relax_all(dref, vref, place, sizes[0] * CX, sizes[1] * CY, sizes[2] * CZ, wet, fields, field_left, damage_out)
    count = part.shape[1]
    advance(part, base_ref, weight, slope, hot, field_left, updated, count - TAIL, TAIL)
    give[0:28, :] = updated[:, count - TAIL :]
    give[28:32, :] = jnp.broadcast_to(counts[0].astype(jnp.float32), (4, TAIL))
    pass_on = pltpu.make_async_remote_copy(
        src_ref=give, dst_ref=take_in, send_sem=send_sem.at[3, 0], recv_sem=recv_sem.at[3, 0],
        device_id={"gz": following}, device_id_type=MESH)
    pass_on.start()
    advance(part, base_ref, weight, slope, hot, field_left, updated, 0, count - TAIL)
    pass_on.wait()
    tail[...] = take_in[...]


def per_device(particles, stencil_base, weights, gradients, counts):
    count = particles.shape[1]
    sizes = tuple(lax.axis_size(a) for a in ("gx", "gy", "gz"))
    vmem = pl.BlockSpec(memory_space=pltpu.VMEM)
    f32 = jnp.float32
    updated, tail, flat_damage = pl.pallas_call(
        functools.partial(step_kernel, sizes),
        name="step",
        out_shape=(
            jax.ShapeDtypeStruct((28, count), f32),
            jax.ShapeDtypeStruct((32, TAIL), f32),
            jax.ShapeDtypeStruct((CX, LW), f32),
        ),
        in_specs=[vmem] * 4 + [pl.BlockSpec(memory_space=pltpu.SMEM)],
        out_specs=(vmem,) * 3,
        scratch_shapes=[
            pltpu.VMEM((NB, count), jnp.bfloat16),
            pltpu.VMEM((32, count), f32),
            pltpu.VMEM(((CX + 2) * 64, count), jnp.bfloat16),
            pltpu.VMEM((CX + 2, 8, LW), f32),
            pltpu.VMEM((3 * RD, LW), f32),
            pltpu.VMEM((3 * RV, LW), f32),
            pltpu.VMEM((3 * RD, LW), f32),
            pltpu.VMEM((64, LW), f32),
            pltpu.VMEM(((CX + 2) * 16, NB), f32),
            pltpu.VMEM((2, XROWS, XB - XA), f32),
            pltpu.VMEM((2, XROWS, XB - XA), f32),
            pltpu.VMEM((2, YROWS, YW), f32),
            pltpu.VMEM((2, YROWS, YW), f32),
            pltpu.VMEM((2, 8 * ZT, LW), f32),
            pltpu.VMEM((2, 8 * ZT, LW), f32),
            pltpu.VMEM((32, TAIL), f32),
            pltpu.VMEM((32, TAIL), f32),
            pltpu.SemaphoreType.DMA((4, 2)),
            pltpu.SemaphoreType.DMA((4, 2)),
        ],
        compiler_params=pltpu.CompilerParams(
            collective_id=0, has_side_effects=True, vmem_limit_bytes=60 * 1024 * 1024
        ),
    )(particles, stencil_base, weights, gradients.reshape(24, count), counts)
    damage = flat_damage[:, : SY * SZ].reshape(CX, SY, SZ)[:, H : H + CY, H : H + CZ]
    prior = tail[28, 0].astype(jnp.int32)
    own_count = counts[0]
    buffer_all = jnp.concatenate([tail[:28], updated, jnp.zeros((28, TAIL), f32)], axis=1)
    start = (MOST - prior) * BIN
    window = lax.dynamic_slice_in_dim(buffer_all, start, (NBIN + MOST) * BIN, 1)
    live = (NBIN - own_count + prior) * BIN
    slot = jnp.arange((NBIN + MOST) * BIN, dtype=jnp.int32)
    migrated = jnp.where(slot[None, :] < live, window, jnp.zeros_like(window))
    return (migrated, damage)


def solution(mesh):
    return jax.shard_map(
        per_device,
        mesh=mesh,
        in_specs=(
            P(None, ("gx", "gy", "gz")),
            P(None, ("gx", "gy", "gz")),
            P(None, ("gx", "gy", "gz")),
            P(None, None, ("gx", "gy", "gz")),
            P(("gx", "gy", "gz")),
        ),
        out_specs=(P(None, ("gx", "gy", "gz")), P("gx", "gy", "gz")),
        check_vma=False,
    )
```

```python
import functools
import jax
import jax.numpy as jnp
from jax import lax
from jax.experimental import pallas as pl
from jax.experimental.pallas import tpu as pltpu
from jax.sharding import PartitionSpec as P

CX = 8
CY = 16
CZ = 32
NBIN = 16
BIN = 128
SUBSTEPS = 4
MOST = 8

time_step = 0.1
relax_rate = 0.2
length_sq = 0.6
shear_mod = 1.0
bulk_coef = 1.5
mass_floor = 0.5

MESH = pl.DeviceIdType.MESH


def up_to(value, unit):
    return (value + unit - 1) // unit * unit


H = SUBSTEPS + 1
SX, SY, SZ = CX + 2 * H, CY + 2 * H, CZ + 2 * H
LW = up_to(SY * SZ, 128)
NB = up_to(CY * SZ + CZ + 1, 128)
OFF = (H - 1) * SZ + H - 1
RD = up_to(SX, 8)
DS, VS = SX, CX + 2
DR, VR = up_to(3 * DS, 8), up_to(3 * VS, 16)
XA, XB = (H - 1) * SZ // 128 * 128, up_to((H + 1 + CY) * SZ, 128)
KEEP = H + 1
XROWS = 3 * KEEP + 6
YW = up_to(KEEP * SZ, 128)
YROWS = DR + VR // 2
DT, VT = DR // 8, VR // 8
SLOTS = SZ // KEEP
ZB = (DT + SLOTS - 1) // SLOTS
FOLDS = 3
FW = (CY + 2) // FOLDS * SZ
ZV = up_to(FW, 128)
ZW = ZB * LW + ZV
TAIL = MOST * BIN


def split(value):
    high = value.astype(jnp.bfloat16)
    low = (value - high.astype(jnp.float32)).astype(jnp.bfloat16)
    return high, low


def take(ref, lane0, width):
    a = lane0 // 128 * 128
    span = up_to(lane0 - a + width, 128)
    value = ref[:, a : a + span]
    shift = (span - (lane0 - a)) % span
    if shift:
        value = pltpu.roll(value, shift, 1)
    value = value[:, : up_to(width, 128)]
    lane = lax.broadcasted_iota(jnp.int32, value.shape, 1)
    return jnp.where(lane < width, value, 0.0)


def put_add(ref, lane0, width, value):
    a = lane0 // 128 * 128
    span = max(up_to(lane0 - a + width, 128), value.shape[1])
    extra = span - value.shape[1]
    if extra:
        value = jnp.concatenate([value, jnp.zeros((value.shape[0], extra), jnp.float32)], axis=1)
    if lane0 - a:
        value = pltpu.roll(value, lane0 - a, 1)
    ref[:, a : a + span] += value


def make_onehot(base_ref, hot):
    flat = base_ref[1:2, :] * SZ + base_ref[2:3, :]
    for r in range(0, NB, 128):
        row = lax.broadcasted_iota(jnp.int32, (128, flat.shape[1]), 0) + r
        hot[r : r + 128, :] = (row == flat).astype(jnp.float32).astype(jnp.bfloat16)


def scatter(part, base_ref, weight, slope, hot, coef, left, nodes, dref, vref, xs_low, xs_high):
    count = part.shape[1]
    mass = part[0:1, :]
    scale = -time_step * part[1:2, :]
    coef[...] = jnp.zeros_like(coef)
    coef[0:1, :] = mass
    coef[1:2, :] = mass * part[23:24, :]
    coef[2:3, :] = mass * part[24:25, :]
    coef[3:6, :] = mass * part[2:5, :]
    for j in range(3):
        for i in range(3):
            coef[8 + 8 * j + 3 + i : 8 + 8 * j + 4 + i, :] = scale * part[14 + 3 * i + j : 15 + 3 * i + j, :]
    bx = jnp.broadcast_to(base_ref[0:1, :], (8, count))
    for bc in range(4):
        pair = []
        for a in range(2):
            k = 4 * a + bc
            term = weight[k : k + 1, :] * coef[0:8, :]
            for j in range(3):
                term = term + slope[8 * j + k : 8 * j + k + 1, :] * coef[8 + 8 * j : 16 + 8 * j, :]
            high = term.astype(jnp.bfloat16).astype(jnp.float32)
            pair.append((high, term - high))
        for x in range(CX + 2):
            for s in range(2):
                row = x * 64 + s * 32 + bc * 8
                value = jnp.where(bx == x, pair[0][s], jnp.where(bx == x - 1, pair[1][s], 0.0))
                left[row : row + 8, :] = value.astype(jnp.bfloat16)
    sums = lax.dot_general(left[...], hot[...], (((1,), (1,)), ((), ())), preferred_element_type=jnp.float32)
    sums = sums.reshape(CX + 2, 2, 4, 8, NB)
    sums = sums[:, 0] + sums[:, 1]
    total = None
    for bc in range(4):
        piece = sums[:, bc].reshape((CX + 2) * 8, NB)
        piece = jnp.concatenate([piece, jnp.zeros((piece.shape[0], LW - NB), jnp.float32)], axis=1)
        piece = pltpu.roll(piece, OFF + (bc >> 1) * SZ + (bc & 1), 1)
        total = piece if total is None else total + piece
    for x in range(CX + 2):
        nodes[x] = total[8 * x : 8 * x + 8, :]
    dref[...] = jnp.zeros_like(dref)
    vref[...] = jnp.zeros_like(vref)
    for x in range(CX + 2):
        for c in range(3):
            dref[c * DS + H - 1 + x : c * DS + H + x, :] = nodes[x, c : c + 1, :]
            vref[c * VS + x : c * VS + x + 1, :] = nodes[x, 3 + c : 4 + c, :]
    for c in range(3):
        at = c * DS + H - 1
        xs_high[c * KEEP : (c + 1) * KEEP, :] = dref[at + CX + 2 - KEEP : at + CX + 2, XA:XB]
        xs_low[c * KEEP : (c + 1) * KEEP, :] = dref[at : at + KEEP, XA:XB]
        at = 3 * KEEP + 2 * c
        xs_high[at : at + 2, :] = vref[c * VS + CX : c * VS + CX + 2, XA:XB]
        xs_low[at : at + 2, :] = vref[c * VS : c * VS + 2, XA:XB]


def only(has, value):
    return jnp.where(has, value, jnp.zeros_like(value))


def add_x(dref, vref, from_low, from_high, has_low, has_high, ys_low, ys_high):
    low = only(has_low, from_low[...])
    high = only(has_high, from_high[...])
    for c in range(3):
        dref[c * DS : c * DS + KEEP, XA:XB] += low[c * KEEP : (c + 1) * KEEP]
        dref[c * DS + SX - KEEP : c * DS + SX, XA:XB] += high[c * KEEP : (c + 1) * KEEP]
        at = 3 * KEEP + 2 * c
        vref[c * VS : c * VS + 2, XA:XB] += low[at : at + 2]
        vref[c * VS + CX : c * VS + CX + 2, XA:XB] += high[at : at + 2]
    half = VR // 2
    for ys, d0, v0 in ((ys_high, CY * SZ, (H - 1 + CY) * SZ), (ys_low, (H - 1) * SZ, (H - 1) * SZ)):
        ys[:DR, :] = take(dref.at[:DR], d0, KEEP * SZ)
        near = take(vref, v0, 2 * SZ)
        ys[DR:, 0:128] = near[:half]
        ys[DR:, 128:256] = near[half:]


def lane_z():
    lane = lax.broadcasted_iota(jnp.int32, (8, LW), 1).astype(jnp.float32)
    y = jnp.floor((lane + 0.5) * (1.0 / SZ))
    return lane - SZ * y, y


def in_slot(z, at, width):
    return (z >= at) & (z < at + width)


def spin(value, shift):
    shift = shift % value.shape[1]
    return pltpu.roll(value, shift, 1) if shift else value


def add_y(dref, vref, from_low, from_high, has_low, has_high, zs_low, zs_high):
    for got, has, d0, v0 in (
        (from_low, has_low, 0, (H - 1) * SZ),
        (from_high, has_high, (SY - KEEP) * SZ, (H - 1 + CY) * SZ),
    ):
        put_add(dref.at[:DR], d0, KEEP * SZ, only(has, got[:DR, :]))
        near = jnp.concatenate([got[DR:, 0:128], got[DR:, 128:256]], axis=0)
        put_add(vref, v0, 2 * SZ, only(has, near))
    z, _ = lane_z()
    short = z[:, :ZV]
    for zs, d0, v0 in ((zs_high, CZ, H - 1 + CZ), (zs_low, H - 1, H - 1)):
        for block in range(ZB):
            out = jnp.zeros((8, LW), jnp.float32)
            for s in range(min(SLOTS, DT - block * SLOTS)):
                r = 8 * (block * SLOTS + s)
                value = spin(dref[r : r + 8, :], s * KEEP - d0)
                out = jnp.where(in_slot(z, s * KEEP, KEEP), value, out)
            zs[:, block * LW : (block + 1) * LW] = out
        out = jnp.zeros((8, ZV), jnp.float32)
        for t in range(VT):
            for q in range(FOLDS):
                at = 2 * (t * FOLDS + q)
                value = take(vref.at[8 * t : 8 * t + 8], (H - 1) * SZ + q * FW + v0, FW)
                value = spin(value, at)
                out = jnp.where(in_slot(short, at, 2), value, out)
        zs[:, ZB * LW :] = out


def add_z(dref, vref, from_low, from_high, has_low, has_high):
    z, _ = lane_z()
    short = z[:, :ZV]
    lane = lax.broadcasted_iota(jnp.int32, (8, ZV), 1)
    for got, has, d0, v0 in (
        (from_low, has_low, 0, H - 1),
        (from_high, has_high, SZ - KEEP, H - 1 + CZ),
    ):
        for block in range(ZB):
            whole = only(has, got[:, block * LW : (block + 1) * LW])
            for s in range(min(SLOTS, DT - block * SLOTS)):
                r = 8 * (block * SLOTS + s)
                value = jnp.where(in_slot(z, s * KEEP, KEEP), whole, 0.0)
                dref[r : r + 8, :] += spin(value, d0 - s * KEEP)
        whole = only(has, got[:, ZB * LW :])
        for t in range(VT):
            for q in range(FOLDS):
                at = 2 * (t * FOLDS + q)
                value = jnp.where(in_slot(short, at, 2) & (lane < FW), whole, 0.0)
                value = spin(value, -at)
                put_add(vref.at[8 * t : 8 * t + 8], (H - 1) * SZ + q * FW + v0, FW, value)


def relax_all(dref, vref, place, nodes_x, nodes_y, nodes_z, wet, fields, field_left, damage_out):
    ix, iy, iz = place
    z, y = lane_z()
    z, y = z[0:1], y[0:1]
    gz = z - H + (iz * CZ).astype(jnp.float32)
    gy = y - H + (iy * CY).astype(jnp.float32)
    flat_in = (gz >= 0) & (gz < nodes_z) & (gy >= 0) & (gy < nodes_y) & (y < SY)
    row = lax.broadcasted_iota(jnp.int32, (RD, 1), 0)
    gx = row - H + ix * CX
    row_in = (gx >= 0) & (gx < nodes_x) & (row < SX)
    inside = row_in.astype(jnp.float32) * flat_in.astype(jnp.float32)
    mass = jnp.maximum(dref[0:RD, :], mass_floor)
    damage = dref[DS : DS + RD, :] / mass * inside
    drive = dref[2 * DS : 2 * DS + RD, :] / mass
    wet[0:RD, :] = mass
    wet[RD : 2 * RD, :] = inside
    for _ in range(SUBSTEPS):
        ring = (
            pltpu.roll(damage, 1, 0)
            + pltpu.roll(damage, RD - 1, 0)
            + pltpu.roll(damage, SZ, 1)
            + pltpu.roll(damage, LW - SZ, 1)
            + pltpu.roll(damage, 1, 1)
            + pltpu.roll(damage, LW - 1, 1)
        )
        laplace = ring - 6.0 * damage
        damage = (damage + relax_rate * (length_sq * laplace - damage + 2.0 * (1.0 - damage) * drive)) * inside
    wet[2 * RD : 3 * RD, :] = damage
    damage_out[...] = wet[2 * RD + H : 2 * RD + H + CX, :]
    n = CX + 2
    factor = wet[RD + H - 1 : RD + H - 1 + n, :] / wet[H - 1 : H - 1 + n, :]
    fields[...] = jnp.zeros_like(fields)
    for c in range(3):
        fields[c * 16 : c * 16 + n, :] = vref[c * VS : c * VS + n, :] * factor
    fields[48 : 48 + n, :] = wet[2 * RD + H - 1 : 2 * RD + H - 1 + n, :]
    whole = fields[...]
    for bc in range(4):
        moved = pltpu.roll(whole, LW - OFF - (bc >> 1) * SZ - (bc & 1), 1)[:, :NB]
        for f in range(4):
            for x in range(n):
                r = x * 16 + f * 4 + bc
                field_left[r : r + 1, :] = moved[f * 16 + x : f * 16 + x + 1, :]


def advance(part, base_ref, weight, slope, hot, field_left, out, at, count):
    lanes = slice(at, at + count)
    there = slice(TAIL + at, TAIL + at + count)
    n = CX + 2
    high, low = split(field_left[...])
    got = jnp.dot(high, hot[:, lanes], preferred_element_type=jnp.float32)
    got = got + jnp.dot(low, hot[:, lanes], preferred_element_type=jnp.float32)
    bx = jnp.broadcast_to(base_ref[0:1, lanes], (16, count))
    near = [jnp.zeros((16, count), jnp.float32), jnp.zeros((16, count), jnp.float32)]
    for x in range(n):
        rows = got[16 * x : 16 * x + 16]
        near[0] = jnp.where(bx == x, rows, near[0])
        near[1] = jnp.where(bx == x - 1, rows, near[1])
    w = weight[:, lanes]
    g = [slope[8 * j : 8 * j + 8, lanes] for j in range(3)]
    corner = [jnp.concatenate([near[0][4 * f : 4 * f + 4], near[1][4 * f : 4 * f + 4]], axis=0) for f in range(4)]
    total = lambda v: jnp.sum(v, axis=0, keepdims=True)
    moved = [total(w * corner[i]) for i in range(3)]
    velgrad = [[total(corner[i] * g[j]) for j in range(3)] for i in range(3)]
    damage_node = total(w * corner[3])
    p = lambda r: part[r : r + 1, lanes]
    deform = [[p(5 + 3 * i + j) for j in range(3)] for i in range(3)]
    stretch = [[(1.0 if i == j else 0.0) + time_step * velgrad[i][j] for j in range(3)] for i in range(3)]
    mapped = [
        [stretch[i][0] * deform[0][j] + stretch[i][1] * deform[1][j] + stretch[i][2] * deform[2][j] for j in range(3)]
        for i in range(3)
    ]
    jacobian = (
        mapped[0][0] * (mapped[1][1] * mapped[2][2] - mapped[1][2] * mapped[2][1])
        - mapped[0][1] * (mapped[1][0] * mapped[2][2] - mapped[1][2] * mapped[2][0])
        + mapped[0][2] * (mapped[1][0] * mapped[2][1] - mapped[1][1] * mapped[2][0])
    )
    left = {}
    for i in range(3):
        for j in range(i, 3):
            left[i, j] = mapped[i][0] * mapped[j][0] + mapped[i][1] * mapped[j][1] + mapped[i][2] * mapped[j][2]
            left[j, i] = left[i, j]
    damaged = jnp.maximum(p(23), damage_node)
    degrade = (1.0 - damaged) ** 2
    swell = bulk_coef * (jacobian - 1.0)

    def put(r, value):
        out[r : r + 1, there] = value

    out[0:2, there] = part[0:2, lanes]
    for i in range(3):
        put(2 + i, moved[i])
        put(25 + i, p(25 + i) + time_step * moved[i])
        for j in range(3):
            put(5 + 3 * i + j, mapped[i][j])
            term = shear_mod * (left[i, j] - (1.0 if i == j else 0.0))
            if i == j:
                term = term + swell
            put(14 + 3 * i + j, degrade * term)
    put(23, damaged)
    energy = 0.5 * shear_mod * (left[0, 0] + left[1, 1] + left[2, 2] - 3.0) + 0.5 * bulk_coef * (jacobian - 1.0) ** 2
    put(24, jnp.maximum(p(24), energy))


def step_kernel(
    sizes, part, base_ref, weight, slope, counts, migrated, damage_out,
    hot, coef, left, nodes, dref, vref, wet, fields, field_left,
    sx, rx, sy, ry, sz, rz, ext, tell, told, send_sem, recv_sem,
):
    names = ("gx", "gy", "gz")
    place = [lax.axis_index(a) for a in names]
    has_low = [i > 0 for i in place]
    has_high = [i < n - 1 for i, n in zip(place, sizes)]
    last = sizes[2]
    following, previous = lax.rem(place[2] + 1, last), lax.rem(place[2] + last - 1, last)
    barrier = pltpu.get_barrier_semaphore()
    waits = 2
    for k in range(2):
        for has, other in ((has_low[k], place[k] - 1), (has_high[k], place[k] + 1)):
            @pl.when(has)
            def _(k=k, other=other):
                pl.semaphore_signal(barrier, inc=1, device_id={names[k]: other}, device_id_type=MESH)
            waits = waits + has.astype(jnp.int32)
    for other in (following, previous):
        pl.semaphore_signal(barrier, inc=1, device_id={"gz": other}, device_id_type=MESH)

    make_onehot(base_ref, hot)
    scatter(part, base_ref, weight, slope, hot, coef, left, nodes, dref, vref, sx.at[0], sx.at[1])
    pl.semaphore_wait(barrier, waits)

    def copies(k, src, dst):
        made = []
        for d, other in ((0, place[k] - 1), (1, place[k] + 1)):
            made.append(pltpu.make_async_remote_copy(
                src_ref=src.at[d], dst_ref=dst.at[1 - d], send_sem=send_sem.at[k, d],
                recv_sem=recv_sem.at[k, 1 - d], device_id={names[k]: other}, device_id_type=MESH))
        return made

    def exchange(k, src, dst):
        made = copies(k, src, dst)
        ahead = ((has_low[k], made[0]), (has_high[k], made[1]))
        for has, copy in ahead:
            @pl.when(has)
            def _(copy=copy):
                copy.start()
        for has, copy in ((has_low[k], made[1]), (has_high[k], made[0])):
            @pl.when(has)
            def _(copy=copy):
                copy.wait_recv()
        for has, copy in ahead:
            @pl.when(has)
            def _(copy=copy):
                copy.wait_send()

    exchange(0, sx, rx)
    add_x(dref, vref, rx.at[0], rx.at[1], has_low[0], has_high[0], sy.at[0], sy.at[1])
    exchange(1, sy, ry)
    add_y(dref, vref, ry.at[0], ry.at[1], has_low[1], has_high[1], sz.at[0], sz.at[1])
    exchange(2, sz, rz)
    add_z(dref, vref, rz.at[0], rz.at[1], has_low[2], has_high[2])
    relax_all(dref, vref, place, sizes[0] * CX, sizes[1] * CY, sizes[2] * CZ, wet, fields, field_left, damage_out)
    count = part.shape[1]

    def to_next(src, dst, slot):
        copy = pltpu.make_async_remote_copy(
            src_ref=src, dst_ref=dst, send_sem=send_sem.at[3 + slot, 0], recv_sem=recv_sem.at[3 + slot, 0],
            device_id={"gz": following}, device_id_type=MESH)
        copy.start()
        return copy

    tell[...] = jnp.broadcast_to(counts[0], tell.shape)
    flying = [to_next(tell, told, 0)]
    chunk = TAIL // 2
    for k in (1, 0):
        at = count - TAIL + k * chunk
        advance(part, base_ref, weight, slope, hot, field_left, ext, at, chunk)
        flying.append(to_next(ext.at[:, TAIL + at : TAIL + at + chunk], ext.at[:, k * chunk : (k + 1) * chunk], 1 + k))
    for at in range(0, count - TAIL, chunk):
        advance(part, base_ref, weight, slope, hot, field_left, ext, at, min(chunk, count - TAIL - at))
    ext[:, TAIL + count :] = jnp.zeros((28, TAIL), jnp.float32)
    for copy in flying:
        copy.wait()
    prior = jnp.broadcast_to(told[0:1, :], (28, BIN))
    live = prior + jnp.broadcast_to(count // BIN - counts[0], prior.shape)
    block = lambda j: ext[:, j * BIN : (j + 1) * BIN]
    for j in range(count // BIN + MOST):
        piece = block(MOST + j)
        for p in range(1, MOST + 1):
            piece = jnp.where(prior == p, block(MOST - p + j), piece)
        migrated[:, j * BIN : (j + 1) * BIN] = jnp.where(live > j, piece, 0.0)


def per_device(particles, stencil_base, weights, gradients, counts):
    count = particles.shape[1]
    sizes = tuple(lax.axis_size(a) for a in ("gx", "gy", "gz"))
    vmem = pl.BlockSpec(memory_space=pltpu.VMEM)
    f32 = jnp.float32
    migrated, flat_damage = pl.pallas_call(
        functools.partial(step_kernel, sizes),
        name="step",
        out_shape=(
            jax.ShapeDtypeStruct((28, count + TAIL), f32),
            jax.ShapeDtypeStruct((CX, LW), f32),
        ),
        in_specs=[vmem] * 4 + [pl.BlockSpec(memory_space=pltpu.SMEM)],
        out_specs=(vmem,) * 2,
        scratch_shapes=[
            pltpu.VMEM((NB, count), jnp.bfloat16),
            pltpu.VMEM((32, count), f32),
            pltpu.VMEM(((CX + 2) * 64, count), jnp.bfloat16),
            pltpu.VMEM((CX + 2, 8, LW), f32),
            pltpu.VMEM((up_to(2 * DS + RD, 8), LW), f32),
            pltpu.VMEM((VR, LW), f32),
            pltpu.VMEM((3 * RD, LW), f32),
            pltpu.VMEM((64, LW), f32),
            pltpu.VMEM(((CX + 2) * 16, NB), f32),
            pltpu.VMEM((2, XROWS, XB - XA), f32),
            pltpu.VMEM((2, XROWS, XB - XA), f32),
            pltpu.VMEM((2, YROWS, YW), f32),
            pltpu.VMEM((2, YROWS, YW), f32),
            pltpu.VMEM((2, 8, ZW), f32),
            pltpu.VMEM((2, 8, ZW), f32),
            pltpu.VMEM((28, count + 2 * TAIL), f32),
            pltpu.VMEM((8, 128), jnp.int32),
            pltpu.VMEM((8, 128), jnp.int32),
            pltpu.SemaphoreType.DMA((6, 2)),
            pltpu.SemaphoreType.DMA((6, 2)),
        ],
        compiler_params=pltpu.CompilerParams(
            collective_id=0, has_side_effects=True, vmem_limit_bytes=60 * 1024 * 1024
        ),
    )(particles, stencil_base, weights, gradients.reshape(24, count), counts)
    damage = flat_damage[:, : SY * SZ].reshape(CX, SY, SZ)[:, H : H + CY, H : H + CZ]
    return (migrated, damage)


def solution(mesh):
    return jax.shard_map(
        per_device,
        mesh=mesh,
        in_specs=(
            P(None, ("gx", "gy", "gz")),
            P(None, ("gx", "gy", "gz")),
            P(None, ("gx", "gy", "gz")),
            P(None, None, ("gx", "gy", "gz")),
            P(("gx", "gy", "gz")),
        ),
        out_specs=(P(None, ("gx", "gy", "gz")), P("gx", "gy", "gz")),
        check_vma=False,
    )
```
